32 devices in a mesh: section: 4 (over x, core), replica: 4 (over z), tensor: 2 (over y).
Axes of the slice: x: 2, y: 2, z: 4, core: 2. Of those that a mesh axis runs over, the one named last changes fastest.
Arguments:
- out_grad: bfloat16 [4, 8, 128, 1024], P('replica', None, 'tensor'), may hold values from -6 to 6
- relu_mask: int32 [4, 4, 8, 128, 4096], P('section', 'replica', None, None, 'tensor'), may hold values from 0 to 255
- w_in: bfloat16 [4, 1024, 32768], P('section', None, 'tensor'), may hold values from -0.1875 to 0.1875
- w_out: bfloat16 [4, 32768, 1024], P('section', 'tensor'), may hold values from -0.03125 to 0.03125
- route: int32 [3, 8, 4], replicated, may hold values from 0 to 3, each once within a row
Outputs:
- in_grads: bfloat16 [4, 4, 8, 128, 1024], P('section', 'replica', None, 'tensor')
The draws below stay inside these ranges and needn't reach their ends.
Inputs may be any that keep to these rules, and one draw needn't show every extreme that they name: Each route[s, m, :] is a permutation of the replicas.
All inputs are finite; a program needn't handle non-finite values.
Results may differ from the reference program's by a relative error of at most 0.0095.
Values may be sent and summed in bfloat16 or wider, within the bound.
A program may use at most 192 MiB of HBM per device.

```python
import jax
import jax.numpy as jnp

D = 1024
FF = 32768
MB = 128
MICRO = 8
WORDS = 4096
N_SECTION = 4
N_REPLICA = 4


def touch_ends(result, key, smallest, high):
    spot = [jax.random.randint(jax.random.fold_in(key, axis), (), 0, length) for axis, length in enumerate(result.shape)]
    main_axis = result.shape.index(max(result.shape))
    neighbour = spot[:main_axis] + [(spot[main_axis] + 1) % result.shape[main_axis]] + spot[main_axis + 1:]
    return result.at[tuple(spot)].set(smallest).at[tuple(neighbour)].set(high)


def shard_levels(own_key, shape, cuts, least, high):
    factor_of, own = 1.0, jax.random.fold_in(own_key, 6)
    for axis_at, blocks in cuts:
        heights = jnp.exp(jax.random.uniform(jax.random.fold_in(own, axis_at), (blocks,), jnp.float32, least / len(cuts), high / len(cuts)))
        factor_of = factor_of * jnp.repeat(heights, shape[axis_at] // blocks).reshape([-1 if axis == axis_at else 1 for axis in range(len(shape))])
    return factor_of


def noise(rng, shape, scale, limit, pieces=(), kind=jnp.bfloat16):
    entries = scale * jax.random.normal(rng, shape, jnp.float32)
    if pieces:
        entries = entries * shard_levels(rng, shape, pieces, -0.22, 0.18)
    return jnp.clip(entries, -limit, limit).astype(kind)


def setup_inputs(seed: int = 0) -> dict:
    splits = jax.random.split(jax.random.key(seed), 6)
    return {
        "out_grad": noise(splits[0], (N_REPLICA, MICRO, MB, D), 1.0, 6.0, ((0, 4), (2, 2))),
        "relu_mask": touch_ends(jax.random.randint(splits[1], (N_SECTION, N_REPLICA, MICRO, MB, WORDS), 0, 256), jax.random.fold_in(splits[1], 1), 0, 255).astype(jnp.int32),
        "w_in": noise(splits[2], (N_SECTION, D, FF), D ** -0.5, 0.1875, ((0, 4), (2, 2))),
        "w_out": noise(splits[3], (N_SECTION, FF, D), FF ** -0.5, 0.03125, ((0, 4), (1, 2))),
        "route": jax.vmap(lambda own: jax.random.permutation(own, N_REPLICA))(jax.random.split(splits[4], (N_SECTION - 1) * MICRO)).reshape((N_SECTION - 1, MICRO, N_REPLICA)).astype(jnp.int32),
    }


def unpack_bits(words):
    shifts = jnp.arange(8, dtype=jnp.int32)
    bits = jnp.right_shift(words[..., None], shifts) & 1
    return bits.reshape(words.shape[:-1] + (words.shape[-1] * 8,))


def reference(out_grad, relu_mask, w_in, w_out, route):
    incoming = out_grad
    results = []
    for section in reversed(range(N_SECTION)):
        flat = incoming.reshape(-1, D)
        pre = jnp.dot(flat, w_out[section].T, preferred_element_type=jnp.float32)
        masked = unpack_bits(relu_mask[section].reshape(-1, WORDS))
        hidden = jnp.where(masked != 0, pre, jnp.float32(0.0)).astype(jnp.bfloat16)
        term = jnp.dot(hidden, w_in[section].T, preferred_element_type=jnp.float32)
        grads = (flat.astype(jnp.float32) + term).astype(jnp.bfloat16).reshape(incoming.shape)
        results.append(grads)
        if section > 0:
            table = route[section - 1]
            slots = jnp.arange(N_REPLICA, dtype=jnp.int32)
            onehot = (table[:, :, None] == slots[None, None, :]).astype(jnp.float32)
            incoming = jnp.einsum("msq,smnd->qmnd", onehot, grads.astype(jnp.float32)).astype(jnp.bfloat16)
    return jnp.stack(results[::-1])
```

```python
import functools

import jax
import jax.numpy as jnp
from jax import lax
from jax.experimental import pallas as pl
from jax.experimental.pallas import tpu as pltpu
from jax.sharding import PartitionSpec as P

PAIR = 2
BITS = 8
SLOTS = 3
MESH = pl.DeviceIdType.MESH


def relay_kernel(
    sizes, route_ref, grad_ref, mask_ref, w_in_ref, w_out_ref, out_ref,
    kept_out, kept_in, flow_out, flow_in, words_buf, xt, hid_a, hid_b, acc, total,
    parts, shares, peers, arrived, final, forward,
    kept_sem, flow_sem, words_sem, entry_sem, result_sem,
    parts_send, parts_recv, peers_send, peers_recv, relay_send, relay_recv, forward_send,
):
    n_section, n_replica, n_tensor, groups, pairs, block, chunk = sizes
    section = lax.axis_index("section")
    replica = lax.axis_index("replica")
    tensor = lax.axis_index("tensor")
    last = n_section - 1
    rows, width = final.shape[1:]
    part_rows = rows // PAIR
    tokens = n_tensor * rows
    words = block // BITS
    turns = groups * pairs

    def kept_copies(j):
        start = pl.multiple_of(j * 2 * block, block)
        return (
            pltpu.make_async_copy(w_out_ref.at[pl.ds(start, block), :], kept_out.at[j], kept_sem.at[j, 0]),
            pltpu.make_async_copy(w_in_ref.at[:, pl.ds(start, block)], kept_in.at[j], kept_sem.at[j, 1]),
        )

    def flow_copies(turn):
        slot = lax.rem(turn, SLOTS)
        start = pl.multiple_of((lax.rem(turn, pairs) * 2 + 1) * block, block)
        return (
            pltpu.make_async_copy(w_out_ref.at[pl.ds(start, block), :], flow_out.at[slot], flow_sem.at[slot, 0]),
            pltpu.make_async_copy(w_in_ref.at[:, pl.ds(start, block)], flow_in.at[slot], flow_sem.at[slot, 1]),
        )

    def words_copy(turn):
        slot = lax.rem(turn, SLOTS)
        first = pl.multiple_of(lax.div(turn, pairs) * PAIR, PAIR)
        start = pl.multiple_of(lax.rem(turn, pairs) * 2 * words, 2 * words)
        return pltpu.make_async_copy(
            mask_ref.at[pl.ds(first, PAIR), :, pl.ds(start, 2 * words)], words_buf.at[slot], words_sem.at[slot]
        )

    bridged = n_replica == 4

    def band(p):
        return pl.ds(p * part_rows, part_rows)

    def parts_copy(g, p, source, target):
        return pltpu.make_async_remote_copy(
            src_ref=parts.at[g, source, band(p), :], dst_ref=parts.at[g, source, band(p), :],
            send_sem=parts_send.at[g, p, target], recv_sem=parts_recv.at[g, p, source],
            device_id=(section, replica, target), device_id_type=MESH,
        )

    def peers_copy(g, p, source, target):
        return pltpu.make_async_remote_copy(
            src_ref=shares.at[g, target, band(p), :], dst_ref=peers.at[g, source, band(p), :],
            send_sem=peers_send.at[g, p, target], recv_sem=peers_recv.at[g, p, source],
            device_id=(section, replica, target), device_id_type=MESH,
        )

    def relay_copy(g, p, i, source, to_section, target):
        return pltpu.make_async_remote_copy(
            src_ref=final.at[g, band(p), :], dst_ref=arrived.at[g, source, band(p), :],
            send_sem=relay_send.at[g, p, i], recv_sem=relay_recv.at[g, p, source],
            device_id=(to_section, target, tensor), device_id_type=MESH,
        )

    def forward_copy(g, p, slot, target):
        return pltpu.make_async_remote_copy(
            src_ref=forward.at[g, band(p), :], dst_ref=arrived.at[g, slot, band(p), :],
            send_sem=forward_send.at[g, p], recv_sem=relay_recv.at[g, p, slot],
            device_id=(section, target, tensor), device_id_type=MESH,
        )

    if bridged:
        low = replica < 2
        inner = (replica == 1) | (replica == 2)
        partner = jnp.where(lax.rem(replica, 2) == 0, replica + 1, replica - 1)
        far = jnp.where(low, 2, 0)
        far_slot = jnp.where(low, 2, 1)
        targets = [jnp.int32(1), jnp.int32(2), jnp.where(low, 0, 3)]
    else:
        inner = True
        targets = [lax.rem(replica + d, n_replica) for d in range(n_replica)]

    def entry_copy(g):
        return pltpu.make_async_copy(grad_ref.at[g], parts.at[g, tensor], entry_sem.at[g])

    def result_copy(g):
        return pltpu.make_async_copy(final.at[g], out_ref.at[g], result_sem.at[g])

    def others():
        return [lax.rem(tensor + d, n_tensor) for d in range(1, n_tensor)]

    table = jnp.minimum(section, last - 1)

    def gathered(g, p, terms, target):
        picked = jnp.zeros((part_rows, width), jnp.float32)
        for slot, sources in terms:
            chosen = 0.0
            for r in sources:
                chosen = chosen + jnp.where(route_ref[table, g * PAIR + p, r] == target, 1.0, 0.0)
            picked = picked + chosen * arrived[g, slot, band(p), :].astype(jnp.float32)
        return picked.astype(jnp.bfloat16)

    def land(g, p, slot):
        relay_copy(g, p, 0, slot, section, replica).wait_recv()

    def pass_on(g, p):
        if not bridged:
            return

        @pl.when((section < last) & inner)
        def _():
            for r in range(n_replica):
                land(g, p, r)
            forward[g, band(p), :] = gathered(g, p, [(far, [far]), (far + 1, [far + 1])], partner)
            forward_copy(g, p, far_slot, partner).start()

    def bring(g, p):
        def give():
            for peer in others():
                parts_copy(g, p, tensor, peer).start()

        @pl.when((section < last) & inner)
        def _():
            if not bridged:
                for r in range(n_replica):
                    land(g, p, r)
            parts[g, tensor, band(p), :] = gathered(g, p, [(r, [r]) for r in range(n_replica)], replica)
            give()

        if bridged:
            @pl.when((section < last) & jnp.logical_not(inner))
            def _():
                for slot in (replica, partner, far_slot):
                    land(g, p, slot)
                parts[g, tensor, band(p), :] = gathered(
                    g, p, [(replica, [replica]), (partner, [partner]), (far_slot, [far, far + 1])], replica
                )
                give()

    def finish(g, p):
        for peer in others():
            peers_copy(g, p, peer, peer).wait_recv()
        start = pl.multiple_of(tensor * rows + p * part_rows, part_rows)
        summed = total[pl.ds(start, part_rows), :]
        for peer in others():
            summed = summed + peers[g, peer, band(p), :].astype(jnp.float32)
        final[g, band(p), :] = (parts[g, tensor, band(p), :].astype(jnp.float32) + summed).astype(jnp.bfloat16)

        @pl.when(section > 0)
        def _():
            for i, target in enumerate(targets):
                relay_copy(g, p, i, replica, section - 1, target).start()

        if p == PAIR - 1:
            result_copy(g).start()

    bit = jnp.left_shift(1, lax.broadcasted_iota(jnp.int32, (1, BITS, tokens), 1))

    def word_rows(slot, half):
        pieces = [
            words_buf[slot, p, t * part_rows:(t + 1) * part_rows, half * words:(half + 1) * words]
            for t in range(n_tensor) for p in range(PAIR)
        ]
        return jnp.concatenate(pieces, axis=0).T

    def half_step(w_out, slot, half, hidden_to, w_in=None, hidden_from=None):
        packed = word_rows(slot, half)
        pieces = block // chunk
        strip = width // pieces
        for c in range(pieces):
            pre = jnp.dot(w_out[c * chunk:(c + 1) * chunk, :], xt[...], preferred_element_type=jnp.float32)
            if w_in is not None:
                acc[c * strip:(c + 1) * strip, :] += jnp.dot(
                    w_in[c * strip:(c + 1) * strip, :], hidden_from[...], preferred_element_type=jnp.float32
                )
            near = packed[c * chunk // BITS:(c + 1) * chunk // BITS]
            keep = (near[:, None, :] & bit) != 0
            hidden = jnp.where(keep, pre.reshape(chunk // BITS, BITS, tokens), 0.0)
            hidden_to[c * chunk:(c + 1) * chunk, :] = hidden.reshape(chunk, tokens).astype(jnp.bfloat16)

    @pl.when(section == last)
    def _():
        for g in range(groups):
            entry_copy(g).start()

    for j in range(pairs):
        for copy in kept_copies(j):
            copy.start()
        if j < 2:
            words_copy(j).start()
            for copy in flow_copies(j):
                copy.start()

    barrier = pltpu.get_barrier_semaphore()
    if bridged:
        pl.semaphore_signal(barrier, inc=1, device_id=(section, partner, tensor), device_id_type=MESH)
    for peer in others():
        pl.semaphore_signal(barrier, inc=1, device_id=(section, replica, peer), device_id_type=MESH)

    @pl.when(section > 0)
    def _():
        for target in range(n_replica):
            pl.semaphore_signal(barrier, inc=1, device_id=(section - 1, target, tensor), device_id_type=MESH)

    @pl.when(section < last)
    def _():
        for target in range(n_replica):
            pl.semaphore_signal(barrier, inc=1, device_id=(section + 1, target, tensor), device_id_type=MESH)

    greeted = n_tensor - 1 + (1 if bridged else 0)
    greeted = greeted + jnp.where(section > 0, n_replica, 0) + jnp.where(section < last, n_replica, 0)
    pl.semaphore_wait(barrier, greeted)

    @pl.when(section == last)
    def _():
        for g in range(groups):
            entry_copy(g).wait()
            for p in range(PAIR):
                for peer in others():
                    parts_copy(g, p, tensor, peer).start()

    for p in range(PAIR):
        pass_on(0, p)
    for p in range(PAIR):
        bring(0, p)
    finish_at = [min(p, pairs - 1) for p in range(PAIR)]
    pass_at = [max(pairs - 2 - PAIR + p, 0) for p in range(PAIR)]
    bring_at = [max(pairs - 1 - PAIR + p, 0) for p in range(PAIR)]

    @pl.loop(0, groups)
    def _(g):
        for p in range(PAIR):
            for peer in others():
                parts_copy(g, p, peer, peer).wait_recv()
        xt[...] = parts[g].reshape(tokens, width).T
        acc[...] = jnp.zeros_like(acc)

        @pl.loop(0, pairs)
        def _(j):
            turn = g * pairs + j
            slot = lax.rem(turn, SLOTS)
            before = lax.rem(turn + SLOTS - 1, SLOTS)
            words_copy(turn).wait()

            @pl.when(g == 0)
            def _():
                for copy in kept_copies(j):
                    copy.wait()

            @pl.when(j == 0)
            def _():
                half_step(kept_out.at[j], slot, 0, hid_a)

            @pl.when(j > 0)
            def _():
                half_step(kept_out.at[j], slot, 0, hid_a, flow_in.at[before], hid_b)

            @pl.when(turn + 2 < turns)
            def _():
                words_copy(turn + 2).start()
                for copy in flow_copies(turn + 2):
                    copy.start()

            for copy in flow_copies(turn):
                copy.wait()
            half_step(flow_out.at[slot], slot, 1, hid_b, kept_in.at[j], hid_a)

            for p in range(PAIR):
                @pl.when((j == finish_at[p]) & (g > 0))
                def _():
                    finish(g - 1, p)

            for p in range(PAIR):
                @pl.when((j == pass_at[p]) & (g + 1 < groups))
                def _():
                    pass_on(g + 1, p)

            for p in range(PAIR):
                @pl.when((j == bring_at[p]) & (g + 1 < groups))
                def _():
                    bring(g + 1, p)

        final_slot = lax.rem(g * pairs + pairs - 1, SLOTS)
        acc[...] += jnp.dot(flow_in[final_slot], hid_b[...], preferred_element_type=jnp.float32)
        total[...] = acc[...].T
        shares[g] = total[...].reshape(n_tensor, rows, width).astype(jnp.bfloat16)
        for p in range(PAIR):
            for peer in others():
                peers_copy(g, p, tensor, peer).start()

    for p in range(PAIR):
        finish(groups - 1, p)

    for g in range(groups):
        result_copy(g).wait()
        for p in range(PAIR):
            for peer in others():
                parts_copy(g, p, tensor, peer).wait_send()
                peers_copy(g, p, tensor, peer).wait_send()

    @pl.when(section > 0)
    def _():
        for g in range(groups):
            for p in range(PAIR):
                for i, target in enumerate(targets):
                    relay_copy(g, p, i, replica, section - 1, target).wait_send()

    if bridged:
        @pl.when((section < last) & inner)
        def _():
            for g in range(groups):
                for p in range(PAIR):
                    forward_copy(g, p, far_slot, partner).wait_send()


def shards(out_grad, relu_mask, w_in, w_out, route):
    n_section = lax.axis_size("section")
    n_replica = lax.axis_size("replica")
    n_tensor = lax.axis_size("tensor")
    micro, part_rows, width = out_grad.shape[1:]
    units = w_out.shape[1]
    groups = micro // PAIR
    rows = PAIR * part_rows
    tokens = n_tensor * rows
    block = min(1024, units // 2)
    chunk = block // 1
    pairs = units // (2 * block)
    words = block // BITS
    bf16, f32, dma = jnp.bfloat16, jnp.float32, pltpu.SemaphoreType.DMA
    sizes = (n_section, n_replica, n_tensor, groups, pairs, block, chunk)
    hbm = pl.BlockSpec(memory_space=pl.ANY)
    results = pl.pallas_call(
        functools.partial(relay_kernel, sizes),
        out_shape=jax.ShapeDtypeStruct((groups, rows, width), bf16),
        in_specs=[pl.BlockSpec(memory_space=pltpu.SMEM), hbm, hbm, hbm, hbm],
        out_specs=hbm,
        scratch_shapes=[
            pltpu.VMEM((pairs, block, width), bf16),
            pltpu.VMEM((pairs, width, block), bf16),
            pltpu.VMEM((SLOTS, block, width), bf16),
            pltpu.VMEM((SLOTS, width, block), bf16),
            pltpu.VMEM((SLOTS, PAIR, n_tensor * part_rows, 2 * words), jnp.int32),
            pltpu.VMEM((width, tokens), bf16),
            pltpu.VMEM((block, tokens), bf16),
            pltpu.VMEM((block, tokens), bf16),
            pltpu.VMEM((width, tokens), f32),
            pltpu.VMEM((tokens, width), f32),
            pltpu.VMEM((groups, n_tensor, rows, width), bf16),
            pltpu.VMEM((groups, n_tensor, rows, width), bf16),
            pltpu.VMEM((groups, n_tensor, rows, width), bf16),
            pltpu.VMEM((groups, n_replica, rows, width), bf16),
            pltpu.VMEM((groups, rows, width), bf16),
            pltpu.VMEM((groups, rows, width), bf16),
            dma((pairs, 2)), dma((SLOTS, 2)), dma((SLOTS,)), dma((groups,)), dma((groups,)),
            dma((groups, PAIR, n_tensor)), dma((groups, PAIR, n_tensor)),
            dma((groups, PAIR, n_tensor)), dma((groups, PAIR, n_tensor)),
            dma((groups, PAIR, n_replica)), dma((groups, PAIR, n_replica)), dma((groups, PAIR)),
        ],
        compiler_params=pltpu.CompilerParams(
            collective_id=0, has_side_effects=True, vmem_limit_bytes=67043328
        ),
        name="relay",
    )(route, out_grad.reshape(groups, rows, width), relu_mask[0, 0], w_in[0], w_out[0])
    return results.reshape(micro, part_rows, width)[None, None]


def solution(mesh):
    in_specs = (
        P("replica", None, "tensor", None),
        P("section", "replica", None, None, "tensor"),
        P("section", None, "tensor"),
        P("section", "tensor", None),
        P(),
    )
    out_specs = P("section", "replica", None, "tensor", None)
    return jax.shard_map(shards, mesh=mesh, in_specs=in_specs, out_specs=out_specs, check_vma=False)
```
